512 devices in a mesh: grid: 32 (over y, z_lo), row: 4 (over x), col: 4 (over z_hi, core).
Axes of the slice: x: 4, y: 8, z: 8 (z_hi: 2, z_lo: 4; z = z_hi * 4 + z_lo), core: 2. Of those that a mesh axis runs over, the one named last changes fastest.
Arguments:
- schur: bfloat16 [32, 4096, 4096], P('grid', 'row', 'col'), may hold values from -6 to 6
- d_inv: bfloat16 [3, 32, 1024, 1024], P(None, 'grid', None, 'col'), may hold values from -0.0009765625 to 0.0087890625, as said below
- blocks: int32 [3, 32, 12], P(None, 'grid'), may hold values from 0 to 15, as said below
Outputs:
- merged: bfloat16 [32, 512, 4096], P('grid', 'row', 'col')
The draws below stay inside these ranges and needn't reach their ends.
Inputs may be any that keep to these rules, and one draw needn't show every extreme that they name: blocks[l, g] is the same for all grids g of one group of 2^l grids at level l. Entry k < 4 lies in k * 4 to (k + 1) * 4 - 1; the other 8 entries are distinct blocks, none of them a pivot block of that list. d_inv[l, g] is the same for all grids g of one group of 2^l grids at level l.
All inputs are finite; a program needn't handle non-finite values.
Results may differ from the reference program's by a relative error of at most 0.0067.
Values may be sent and summed in bfloat16 or wider, within the bound.
No kernel may reach another device: no remote copies, remote signals or barrier semaphores. Data moves between devices by JAX's collectives and lax.ppermute only.
A program may use at most 64 MiB of HBM per device.

```python
import jax
import jax.numpy as jnp
from jax import lax

M = 4096
W = 1024
LISTED = 8
GRIDS = 32
LEVELS = 3
FINAL = 8
PIVOTS = 4
BLOCK = 256
NBLOCKS = 16
N_ROW = 4


def order_for(key, height, grid_pos):
    group_seed = jax.random.fold_in(jax.random.fold_in(key, 1000 + height), grid_pos >> height)
    pivot_key, list_key = jax.random.split(group_seed)
    spacing = NBLOCKS // PIVOTS
    offsets = jax.random.randint(pivot_key, (PIVOTS,), 0, spacing, dtype=jnp.int32)
    pivots = jnp.arange(PIVOTS, dtype=jnp.int32) * spacing + offsets
    scores = jax.random.permutation(list_key, NBLOCKS).astype(jnp.int32)
    numbers = jnp.arange(NBLOCKS, dtype=jnp.int32)
    is_pivot = jnp.any(numbers[:, None] == pivots[None, :], axis=1)
    scores = jnp.where(is_pivot, scores + NBLOCKS, scores)
    listed = jnp.argsort(scores, stable=True)[:LISTED].astype(jnp.int32)
    return jnp.concatenate([pivots, listed]).astype(jnp.int32)


def draw_blocks(key, part):
    grid_ids = jnp.arange(GRIDS, dtype=jnp.int32)
    layers = [jax.vmap(lambda grid_pos: order_for(key, height, grid_pos))(grid_ids) for height in range(LEVELS)]
    return jnp.stack(layers).astype(jnp.int32)


def inverse_for(key, height, grid_pos):
    group_seed = jax.random.fold_in(jax.random.fold_in(key, 2000 + height), grid_pos >> height)
    random_part = jnp.clip(jax.random.normal(group_seed, (W, W), jnp.float32), -4.0, 4.0)
    root = jnp.sqrt(jnp.float32(W))
    return (jnp.eye(W, dtype=jnp.float32) + random_part / root) * (0.25 / root)


def draw_d_inv(key, part):
    grid_ids = jnp.arange(GRIDS, dtype=jnp.int32)
    layers = [jax.vmap(lambda grid_pos: inverse_for(key, height, grid_pos))(grid_ids) for height in range(LEVELS)]
    return jnp.stack(layers).astype(jnp.bfloat16)


def shard_levels(own_key, shape, cuts, smallest, largest):
    loudness = 1.0
    for dim, shards_of in cuts:
        draws = jax.random.uniform(jax.random.fold_in(jax.random.fold_in(own_key, 6), dim), (shards_of,), jnp.float32, smallest / len(cuts), largest / len(cuts))
        loudness = loudness * jnp.repeat(jnp.exp(draws), shape[dim] // shards_of).reshape((-1,) + (1,) * (len(shape) - 1 - dim))
    return loudness


def noise(own_key, dims, width, reach, cuts=(), kind=jnp.bfloat16):
    entries = jax.random.normal(own_key, dims, jnp.float32) * width
    if len(cuts) > 0:
        entries = shard_levels(own_key, dims, cuts, -0.22, 0.18) * entries
    return jnp.clip(entries, min=-reach, max=reach).astype(kind)


def setup_inputs(seed: int = 0) -> dict:
    key_of = jax.random.split(jax.random.key(seed), 4)
    return {
        "schur": noise(key_of[0], (GRIDS, M, M), 1.0, 6.0, ((0, 32), (1, 4), (2, 4))),
        "d_inv": draw_d_inv(jax.random.fold_in(key_of[3], 71), 0),
        "blocks": draw_blocks(jax.random.fold_in(key_of[3], 71), 0),
    }


def eliminate(current, chosen, inverse):
    current = current.astype(jnp.float32)
    within = jnp.arange(BLOCK, dtype=jnp.int32)
    pivot_cols = (chosen[:PIVOTS, None] * BLOCK + within[None, :]).reshape(-1).astype(jnp.int32)
    listed_rows = (chosen[PIVOTS:, None] * BLOCK + within[None, :]).reshape(-1).astype(jnp.int32)
    left_panel = current[listed_rows][:, pivot_cols].astype(jnp.bfloat16).astype(jnp.float32)
    upper_panel = current[pivot_cols][:, listed_rows].astype(jnp.bfloat16).astype(jnp.float32)
    scaled = jnp.dot(left_panel, inverse.astype(jnp.float32), preferred_element_type=jnp.float32)
    scaled = scaled.astype(jnp.bfloat16).astype(jnp.float32)
    change = jnp.dot(scaled, upper_panel, preferred_element_type=jnp.float32)
    spread = jnp.zeros((change.shape[0], current.shape[1]), change.dtype).at[:, listed_rows].set(change)
    updated = current.at[listed_rows].add(-spread)
    return updated.astype(jnp.bfloat16)


def reference(schur, d_inv, blocks):
    stored = schur
    for height in range(LEVELS):
        stride = 2 ** height
        chosen_all = blocks[height, ::stride]
        inverse_all = d_inv[height, ::stride]
        result = lax.map(lambda packed: eliminate(packed[0], packed[1], packed[2]), (stored, chosen_all, inverse_all))
        stored = result[0::2].astype(jnp.float32) + result[1::2].astype(jnp.float32)
    final_tiles = stored.astype(jnp.bfloat16)
    quarter = M // N_ROW
    share_rows = quarter // FINAL
    shaped = final_tiles.reshape(GRIDS // FINAL, N_ROW, FINAL, share_rows, M)
    grid_ids = jnp.arange(GRIDS, dtype=jnp.int32)
    reverse = jnp.zeros((GRIDS,), jnp.int32)
    for height in range(LEVELS):
        reverse = reverse + ((grid_ids >> height) & 1) * (2 ** (LEVELS - 1 - height))
    picked = shaped[grid_ids // FINAL, :, reverse]
    return picked.reshape(GRIDS, M // FINAL, M)
```

```python
import jax
import jax.numpy as jnp
from jax import lax
from jax.experimental import pallas as pl
from jax.experimental.pallas import tpu as pltpu
from jax.sharding import PartitionSpec as P


BF = jnp.bfloat16
F32 = jnp.float32


def move(block, axes, route):
    sizes = [lax.axis_size(a) for a in axes]
    count = 1
    for s in sizes:
        count *= s
    return lax.ppermute(block, axes, [(i, route(i)) for i in range(count)])


def across(block, apart):
    return move(block, ("grid",), lambda i: i ^ apart)


def far_half(block):
    return move(block, ("col",), lambda i: i ^ 2)


def other_core(block):
    return move(block, ("col",), lambda i: i ^ 1)


def row_swap(block, first):
    cols = lax.axis_size("col")

    def route(i):
        r, c = divmod(i, cols)
        mask = 1 if (c % 2 == 0) == first else 3
        return (r ^ mask) * cols + c

    return move(block, ("row", "col"), route)


def arrival(quarter, row, core):
    x = quarter ^ row
    near = jnp.where(core == 0, 1, 3)
    return jnp.where(x == 0, 0, jnp.where(x == 2, 3, jnp.where(x == near, 1, 2)))


def has(blk, level, wanted):
    found = blk[level, 4] == wanted
    for n in range(5, 12):
        found = found | (blk[level, n] == wanted)
    return found


def slot_of(b, pivot):
    return jnp.clip(b - jnp.where(b > pivot, 1, 0), 0, 2)


def block_of(slot, pivot):
    return slot + jnp.where(slot >= pivot, 1, 0)


def row_pivot(blk, pos, level):
    return blk[level, pos[1]] - 4 * pos[1]


def col_pivot(blk, pos, level):
    return blk[level, pos[2]] - 4 * pos[2]


def bit_of(pos, n):
    return (pos[0] >> n) & 1


def call(body, grid, in_specs, out_specs, out_shape, scratch, flops=0, size=0):
    return pl.pallas_call(
        body,
        grid_spec=pltpu.PrefetchScalarGridSpec(
            num_scalar_prefetch=2,
            grid=grid,
            in_specs=in_specs,
            out_specs=out_specs,
            scratch_shapes=scratch,
        ),
        out_shape=out_shape,
        compiler_params=pltpu.CompilerParams(
            dimension_semantics=("arbitrary",) * len(grid), vmem_limit_bytes=32 * 2**20
        ),
        cost_estimate=pl.CostEstimate(flops=flops, bytes_accessed=size, transcendentals=0),
    )


def whole(shape):
    return pl.BlockSpec(shape, lambda *_: (0,) * len(shape))


def out(shape):
    return jax.ShapeDtypeStruct(shape, BF)


def pack(blk, pos, tile):
    def body(blk_ref, pos_ref, left_in, upper_in, left_out, upper_out):
        left_out[0] = left_in[0]
        upper_out[0] = upper_in[0]

    spec = pl.BlockSpec((1, 256, 256), lambda i, blk, pos: (i, 0, 0))
    return call(
        body,
        (3,),
        [
            pl.BlockSpec(
                (1, 256, 256),
                lambda i, blk, pos: (0, block_of(i, row_pivot(blk, pos, 0)), col_pivot(blk, pos, 0)),
            ),
            pl.BlockSpec(
                (1, 256, 256),
                lambda i, blk, pos: (0, row_pivot(blk, pos, 0), block_of(i, col_pivot(blk, pos, 0))),
            ),
        ],
        [spec, spec],
        [out((3, 256, 256)), out((3, 256, 256))],
        [],
        size=2**20,
    )(blk, pos, tile, tile)


def join_inverse(blk, pos, levels, own, far, other, other_far):
    first, count = levels

    def body(blk_ref, pos_ref, dc, dz, oc, oz, d_ref):
        c = pos_ref[2]
        for flip, ref in zip((0, 2, 1, 3), (dc, dz, oc, oz)):
            d_ref[0, :, pl.ds(pl.multiple_of((c ^ flip) * 256, 256), 256)] = ref[0, 0]

    def far_map(flip):
        return lambda n, k, blk, pos: (arrival(k, pos[1], pos[2] % 2 ^ flip), n, 0, 0)

    near = pl.BlockSpec((1, 1, 256, 256), lambda n, k, blk, pos: (first + n, k, 0, 0))
    return call(
        body,
        (count, 4),
        [
            near,
            pl.BlockSpec((1, 1, 256, 256), far_map(0)),
            near,
            pl.BlockSpec((1, 1, 256, 256), far_map(1)),
        ],
        pl.BlockSpec((1, 256, 1024), lambda n, k, blk, pos: (n, k, 0)),
        out((count, 1024, 1024)),
        [],
        size=count * 2**22,
    )(blk, pos, own, far, other, other_far)


def join_upper(blk, pos, pieces):
    parts = len(pieces)
    rows = 256 // parts

    def body(blk_ref, pos_ref, *refs):
        u_all = refs[-1]
        r, c = pos_ref[1], pos_ref[2]
        near_q = r ^ jnp.where(c % 2 == 0, 1, 3)
        far_q = r ^ jnp.where(c % 2 == 0, 3, 1)
        for h in range(parts):
            u0, u1, u2 = refs[3 * h : 3 * h + 3]
            for s in range(3):
                u_all[s, pl.ds(r * 256 + h * rows, rows)] = u0[s]
                u_all[s, pl.ds(near_q * 256 + h * rows, rows)] = u1[s]
                u_all[s, pl.ds(far_q * 256 + h * rows, rows)] = u2[0, s]
                u_all[s, pl.ds((r ^ 2) * 256 + h * rows, rows)] = u2[1, s]

    return call(
        body,
        (1,),
        [whole((3, rows, 256)), whole((3, rows, 256)), whole((2, 3, rows, 256))] * parts,
        whole((3, 1024, 256)),
        out((3, 1024, 256)),
        [],
        size=3 * 2**20,
    )(blk, pos, *[x for piece in pieces for x in piece])


def scale(blk, pos, lane, lefts, inverse):
    rows = lefts[0].shape[0]

    def body(blk_ref, pos_ref, l0, l1, l2, l3, d_ref, s_ref, l_all):
        c = pos_ref[2]

        @pl.when(pl.program_id(0) == 0)
        def _():
            for flip, ref in zip((0, 2, 1, 3), (l0, l1, l2, l3)):
                for i in range(rows):
                    l_all[i * 256 : (i + 1) * 256, pl.ds(pl.multiple_of((c ^ flip) * 256, 256), 256)] = ref[i]

        s_ref[...] = jnp.dot(l_all[...], d_ref[0], preferred_element_type=F32).astype(BF)

    return call(
        body,
        (4,),
        [whole((rows, 256, 256))] * 4
        + [pl.BlockSpec((1, 1024, 256), lambda q, blk, pos: (lane, 0, q))],
        pl.BlockSpec((rows * 256, 256), lambda q, blk, pos: (0, q)),
        out((rows * 256, 1024)),
        [pltpu.VMEM((rows * 256, 1024), BF)],
        flops=2 * rows * 256 * 1024 * 1024,
        size=4 * 2**20,
    )(blk, pos, *lefts, inverse)


def subtract_product(blk_ref, pos_ref, level, row_block, scaled, u_ref, e_all, held):
    c = pos_ref[2]
    pivot = col_pivot(blk_ref, pos_ref, level)
    row_on = has(blk_ref, level, pos_ref[1] * 4 + row_block)
    for s in range(3):
        b = block_of(s, pivot)
        on = row_on & has(blk_ref, level, c * 4 + b)

        @pl.when(on)
        def _():
            change = jnp.dot(scaled(), u_ref[s], preferred_element_type=F32)
            e_all[b] = (held(b, s) - change).astype(BF)

        @pl.when(jnp.logical_not(on))
        def _():
            e_all[b] = held(b, s).astype(BF)


def update_first(blk, pos, tile, scaled, upper):
    def row_block(i, pos):
        bit = bit_of(pos, 0)
        return jnp.where(i < 2, 2 * (1 - bit), 2 * bit) + (i & 1)

    def body(blk_ref, pos_ref, x_ref, s_ref, u_ref, a0, a1, al, b0, b1, ks, kp, e_all):
        i = pl.program_id(0)
        rb = row_block(i, pos_ref)
        for b in range(4):
            e_all[b] = x_ref[0, :, b * 256 : (b + 1) * 256]
        subtract_product(
            blk_ref, pos_ref, 0, rb, lambda: s_ref[...], u_ref, e_all,
            lambda b, s: e_all[b].astype(F32),
        )
        nxt = col_pivot(blk_ref, pos_ref, 1)
        half = i & 1

        for n, b_ref in ((0, b0), (1, b1)):

            @pl.when(i == n)
            def _():
                al[n] = e_all[nxt]
                for d in range(3):
                    b_ref[d] = e_all[block_of(d, nxt)]

        @pl.when(i >= 2)
        def _():
            kp[half] = e_all[nxt]
            for d in range(3):
                ks[half, d] = e_all[block_of(d, nxt)]

        @pl.when(rb == row_pivot(blk_ref, pos_ref, 1))
        def _():
            for d in range(3):
                a0[d] = e_all[block_of(d, nxt), :128]
                a1[d] = e_all[block_of(d, nxt), 128:]

    shapes = [
        (3, 128, 256), (3, 128, 256), (2, 256, 256), (3, 256, 256), (3, 256, 256),
        (2, 3, 256, 256), (2, 256, 256),
    ]
    return call(
        body,
        (4,),
        [
            pl.BlockSpec((1, 256, 1024), lambda i, blk, pos: (0, row_block(i, pos), 0)),
            pl.BlockSpec(
                (256, 1024),
                lambda i, blk, pos: (slot_of(row_block(i, pos), row_pivot(blk, pos, 0)), 0),
            ),
            whole((3, 1024, 256)),
        ],
        [whole(x) for x in shapes],
        [out(x) for x in shapes],
        [pltpu.VMEM((4, 256, 256), BF)],
        flops=2 * 768 * 1024 * 768,
        size=8 * 2**20,
    )(blk, pos, tile, scaled, upper)


def update_second(blk, pos, ks, rb0, rb1, kp, ra, scaled, upper):
    def body(
        blk_ref, pos_ref, ks_ref, rb0_ref, rb1_ref, kp_ref, ra_ref, s_ref, u_ref,
        a0, a1, al, bg, ks2, kp2, e_all,
    ):
        pivot = col_pivot(blk_ref, pos_ref, 1)
        nxt = col_pivot(blk_ref, pos_ref, 2)
        for d in range(3):
            a0[d] = jnp.zeros((128, 256), BF)
            a1[d] = jnp.zeros((128, 256), BF)
        for n, rb_ref in ((0, rb0_ref), (1, rb1_ref)):
            here = 2 * bit_of(pos_ref, 0) + n
            e_all[pivot] = (kp_ref[n].astype(F32) + ra_ref[n].astype(F32)).astype(BF)
            subtract_product(
                blk_ref, pos_ref, 1, here, lambda: s_ref[n * 256 : (n + 1) * 256], u_ref, e_all,
                lambda b, s: ks_ref[n, s].astype(F32) + rb_ref[s].astype(F32),
            )

            @pl.when(bit_of(pos_ref, 1) != n)
            def _():
                al[0] = e_all[nxt]
                for d in range(3):
                    bg[d] = e_all[block_of(d, nxt)]

            @pl.when(bit_of(pos_ref, 1) == n)
            def _():
                kp2[0] = e_all[nxt]
                for d in range(3):
                    ks2[d] = e_all[block_of(d, nxt)]

            @pl.when(here == row_pivot(blk_ref, pos_ref, 2))
            def _():
                for d in range(3):
                    a0[d] = e_all[block_of(d, nxt), :128]
                    a1[d] = e_all[block_of(d, nxt), 128:]

    shapes = [
        (3, 128, 256), (3, 128, 256), (1, 256, 256), (3, 256, 256), (3, 256, 256), (1, 256, 256),
    ]
    return call(
        body,
        (1,),
        [whole(x.shape) for x in (ks, rb0, rb1, kp, ra, scaled, upper)],
        [whole(x) for x in shapes],
        [out(x) for x in shapes],
        [pltpu.VMEM((4, 256, 256), BF)],
        flops=2 * 512 * 1024 * 768,
        size=7 * 2**20,
    )(blk, pos, ks, rb0, rb1, kp, ra, scaled, upper)


def update_third(blk, pos, ks, rb, kp, ra, scaled, upper):
    def body(
        blk_ref, pos_ref, ks_ref, rb_ref, kp_ref, ra_ref, s_ref, u_ref, give, keep, e_all
    ):
        here = 2 * bit_of(pos_ref, 0) + bit_of(pos_ref, 1)
        pivot = col_pivot(blk_ref, pos_ref, 2)
        e_all[pivot] = (kp_ref[0].astype(F32) + ra_ref[0].astype(F32)).astype(BF)
        subtract_product(
            blk_ref, pos_ref, 2, here, lambda: s_ref[...], u_ref, e_all,
            lambda b, s: ks_ref[s].astype(F32) + rb_ref[s].astype(F32),
        )
        bit = bit_of(pos_ref, 2)
        for b in range(4):
            give[:, b * 256 : (b + 1) * 256] = e_all[b, pl.ds((1 - bit) * 128, 128)]
            keep[:, b * 256 : (b + 1) * 256] = e_all[b, pl.ds(bit * 128, 128)]

    return call(
        body,
        (1,),
        [whole(x.shape) for x in (ks, rb, kp, ra, scaled, upper)],
        [whole((128, 1024)), whole((128, 1024))],
        [out((128, 1024)), out((128, 1024))],
        [pltpu.VMEM((4, 256, 256), BF)],
        flops=2 * 256 * 1024 * 768,
        size=4 * 2**20,
    )(blk, pos, ks, rb, kp, ra, scaled, upper)


def total(a, b):
    return (a.astype(F32) + b.astype(F32)).astype(BF)


def spread_rows(piece):
    near = row_swap(piece, True)
    far = row_swap(jnp.stack([piece, near]), False)
    return piece, near, far


def gather_left(piece):
    far = far_half(piece)
    own_other = other_core(piece)
    far_other = other_core(far)
    return piece, far, own_other, far_other


def far_inverse(part):
    arrived = far_half(part)
    near = row_swap(arrived, True)
    two = jnp.stack([arrived, near])
    four = jnp.concatenate([two, row_swap(two, False)])
    return four, other_core(four)


def eliminate(schur, d_inv, blocks):
    row = lax.axis_index("row").astype(jnp.int32)
    blk = blocks[:, 0]
    pos = jnp.stack(
        [lax.axis_index("grid").astype(jnp.int32), row, lax.axis_index("col").astype(jnp.int32)]
    )
    inverse = d_inv.reshape(3, 4, 256, 256)
    quarter = lax.dynamic_index_in_dim(inverse, row, 1, keepdims=False)

    dz0, oz0 = far_inverse(quarter[:1])
    left0, upper0 = pack(blk, pos, schur)
    d_other = other_core(inverse)
    upper0 = join_upper(blk, pos, [spread_rows(upper0)])
    lefts0 = gather_left(left0)
    dz12, oz12 = far_inverse(quarter[1:])
    whole0 = join_inverse(blk, pos, (0, 1), inverse, dz0, d_other, oz0)
    whole12 = join_inverse(blk, pos, (1, 2), inverse, dz12, d_other, oz12)

    scaled0 = scale(blk, pos, 0, lefts0, whole0)
    a0, a1, al, b0, b1, ks, kp = update_first(blk, pos, schur, scaled0, upper0)
    u10 = total(a0, across(a0, 1))
    ral = across(al, 1)
    u11 = total(a1, across(a1, 1))
    rb0 = across(b0, 1)
    rb1 = across(b1, 1)
    upper1 = join_upper(blk, pos, [spread_rows(u10), spread_rows(u11)])
    lefts1 = gather_left(total(kp, ral))
    scaled1 = scale(blk, pos, 0, lefts1, whole12)
    a0, a1, al, bg, ks, kp = update_second(blk, pos, ks, rb0, rb1, kp, ral, scaled1, upper1)

    u20 = total(a0, across(a0, 2))
    u21 = total(a1, across(a1, 2))
    ral = across(al, 2)
    rb = across(bg, 2)
    u20 = total(u20, across(u20, 1))
    u21 = total(u21, across(u21, 1))
    upper2 = join_upper(blk, pos, [spread_rows(u20), spread_rows(u21)])
    lefts2 = gather_left(total(kp, ral))
    scaled2 = scale(blk, pos, 1, lefts2, whole12)
    give, keep = update_third(blk, pos, ks, rb, kp, ral, scaled2, upper2)
    return total(keep, across(give, 4))[None]


def solution(mesh):
    return jax.shard_map(
        eliminate,
        mesh=mesh,
        in_specs=(P("grid", "row", "col"), P(None, "grid", None, "col"), P(None, "grid", None)),
        out_specs=P("grid", "row", "col"),
        check_vma=False,
    )
```

```python
import jax
import jax.numpy as jnp
from jax import lax
from jax.experimental import pallas as pl
from jax.experimental.pallas import tpu as pltpu
from jax.sharding import PartitionSpec as P


BF = jnp.bfloat16
F32 = jnp.float32


def move(block, axes, route):
    sizes = [lax.axis_size(a) for a in axes]
    count = 1
    for s in sizes:
        count *= s
    return lax.ppermute(block, axes, [(i, route(i)) for i in range(count)])


def across(block, apart):
    return move(block, ("grid",), lambda i: i ^ apart)


def far_half(block):
    return move(block, ("col",), lambda i: i ^ 2)


def other_core(block):
    return move(block, ("col",), lambda i: i ^ 1)


def row_swap(block, first):
    cols = lax.axis_size("col")

    def route(i):
        r, c = divmod(i, cols)
        mask = 1 if (c % 2 == 0) == first else 3
        return (r ^ mask) * cols + c

    return move(block, ("row", "col"), route)


def arrival(quarter, row, core):
    x = quarter ^ row
    near = jnp.where(core == 0, 1, 3)
    return jnp.where(x == 0, 0, jnp.where(x == 2, 3, jnp.where(x == near, 1, 2)))


def has(blk, level, wanted):
    found = blk[level, 4] == wanted
    for n in range(5, 12):
        found = found | (blk[level, n] == wanted)
    return found


def slot_of(b, pivot):
    return jnp.clip(b - jnp.where(b > pivot, 1, 0), 0, 2)


def block_of(slot, pivot):
    return slot + jnp.where(slot >= pivot, 1, 0)


def row_pivot(blk, pos, level):
    return blk[level, pos[1]] - 4 * pos[1]


def col_pivot(blk, pos, level):
    return blk[level, pos[2]] - 4 * pos[2]


def bit_of(pos, n):
    return (pos[0] >> n) & 1


def call(body, grid, in_specs, out_specs, out_shape, scratch, flops=0, size=0):
    return pl.pallas_call(
        body,
        grid_spec=pltpu.PrefetchScalarGridSpec(
            num_scalar_prefetch=2,
            grid=grid,
            in_specs=in_specs,
            out_specs=out_specs,
            scratch_shapes=scratch,
        ),
        out_shape=out_shape,
        compiler_params=pltpu.CompilerParams(
            dimension_semantics=("arbitrary",) * len(grid), vmem_limit_bytes=16 * 2**20
        ),
        cost_estimate=pl.CostEstimate(flops=flops, bytes_accessed=size, transcendentals=0),
    )


def whole(shape):
    return pl.BlockSpec(shape, lambda *_: (0,) * len(shape))


def out(shape):
    return jax.ShapeDtypeStruct(shape, BF)


def pack(blk, pos, tile, inverse):
    def body(blk_ref, pos_ref, left_in, upper_in, quarter_in, left_out, upper_out, first, later):
        left_out[0] = left_in[0]
        upper_out[0] = upper_in[0]

        @pl.when(pl.program_id(0) == 0)
        def _():
            first[0] = quarter_in[0, 0]

        @pl.when(pl.program_id(0) > 0)
        def _():
            later[0] = quarter_in[0, 0]

    spec = pl.BlockSpec((1, 256, 256), lambda i, blk, pos: (i, 0, 0))
    return call(
        body,
        (3,),
        [
            pl.BlockSpec(
                (1, 256, 256),
                lambda i, blk, pos: (0, block_of(i, row_pivot(blk, pos, 0)), col_pivot(blk, pos, 0)),
            ),
            pl.BlockSpec(
                (1, 256, 256),
                lambda i, blk, pos: (0, row_pivot(blk, pos, 0), block_of(i, col_pivot(blk, pos, 0))),
            ),
            pl.BlockSpec((1, 1, 256, 256), lambda i, blk, pos: (i, pos[1], 0, 0)),
        ],
        [
            spec,
            spec,
            whole((1, 256, 256)),
            pl.BlockSpec((1, 256, 256), lambda i, blk, pos: (jnp.maximum(i - 1, 0), 0, 0)),
        ],
        [out((3, 256, 256)), out((3, 256, 256)), out((1, 256, 256)), out((2, 256, 256))],
        [],
        size=2**21,
    )(blk, pos, tile, tile, inverse)


def join_inverse(blk, pos, levels, own, far, other, other_far):
    first, count = levels

    def body(blk_ref, pos_ref, dc, dz, oc, oz, d_ref):
        r, c = pos_ref[1], pos_ref[2]
        for k in range(4):
            rows = slice(k * 256, (k + 1) * 256)
            for flip, piece in (
                (0, dc[0, k]),
                (2, dz[arrival(k, r, c % 2), 0]),
                (1, oc[0, k]),
                (3, oz[arrival(k, r, (c % 2) ^ 1), 0]),
            ):
                d_ref[0, rows, pl.ds(pl.multiple_of((c ^ flip) * 256, 256), 256)] = piece

    near = pl.BlockSpec((1, 4, 256, 256), lambda n, blk, pos: (first + n, 0, 0, 0))
    swapped = pl.BlockSpec((4, 1, 256, 256), lambda n, blk, pos: (0, n, 0, 0))
    return call(
        body,
        (count,),
        [near, swapped, near, swapped],
        pl.BlockSpec((1, 1024, 1024), lambda n, blk, pos: (n, 0, 0)),
        out((count, 1024, 1024)),
        [],
        size=count * 2**22,
    )(blk, pos, own, far, other, other_far)


def join_upper(blk, pos, pieces, halved=False):
    def body(blk_ref, pos_ref, *refs):
        r, c = pos_ref[1], pos_ref[2]
        u_all = refs[-1]
        lead = bit_of(pos_ref, 0) * 128
        if len(refs) == 5:
            parts = tuple(((r + n) & 3, ref) for n, ref in zip((0, 2, 3, 1), refs))
        else:
            near_q = r ^ jnp.where(c % 2 == 0, 1, 3)
            far_q = r ^ jnp.where(c % 2 == 0, 3, 1)
            parts = (r, refs[0]), (near_q, refs[1]), (far_q, refs[2].at[0]), (r ^ 2, refs[2].at[1])
        for q, ref in parts:
            for s in range(3):
                if halved:
                    u_all[s, pl.ds(q * 256 + lead, 128)] = ref[s, :128]
                    u_all[s, pl.ds(q * 256 + 128 - lead, 128)] = ref[s, 128:]
                else:
                    u_all[s, pl.ds(q * 256, 256)] = ref[s]

    return call(
        body,
        (1,),
        [whole(x.shape) for x in pieces],
        whole((3, 1024, 256)),
        out((3, 1024, 256)),
        [],
        size=3 * 2**20,
    )(blk, pos, *pieces)


def scale(blk, pos, lane, lefts, inverse):
    rows = lefts[0].shape[1]

    def body(blk_ref, pos_ref, own, other, d_ref, s_ref, l_all):
        c = pos_ref[2]

        @pl.when(pl.program_id(0) == 0)
        def _():
            for flip, ref in zip((0, 2, 1, 3), (own.at[0], own.at[1], other.at[0], other.at[1])):
                for i in range(rows):
                    l_all[i * 256 : (i + 1) * 256, pl.ds(pl.multiple_of((c ^ flip) * 256, 256), 256)] = ref[i]

        s_ref[...] = jnp.dot(l_all[...], d_ref[0], preferred_element_type=F32).astype(BF)

    return call(
        body,
        (4,),
        [whole((2, rows, 256, 256))] * 2
        + [pl.BlockSpec((1, 1024, 256), lambda q, blk, pos: (lane, 0, q))],
        pl.BlockSpec((rows * 256, 256), lambda q, blk, pos: (0, q)),
        out((rows * 256, 1024)),
        [pltpu.VMEM((rows * 256, 1024), BF)],
        flops=2 * rows * 256 * 1024 * 1024,
        size=4 * 2**20,
    )(blk, pos, *lefts, inverse)


def subtract_product(blk_ref, pos_ref, level, row_block, scaled, u_ref, e_all, held):
    c = pos_ref[2]
    pivot = col_pivot(blk_ref, pos_ref, level)
    row_on = has(blk_ref, level, pos_ref[1] * 4 + row_block)
    for s in range(3):
        b = block_of(s, pivot)
        on = row_on & has(blk_ref, level, c * 4 + b)

        @pl.when(on)
        def _():
            change = jnp.dot(scaled(), u_ref[s], preferred_element_type=F32)
            e_all[b] = (held(b, s) - change).astype(BF)

        @pl.when(jnp.logical_not(on))
        def _():
            e_all[b] = held(b, s).astype(BF)


def update_first(blk, pos, tile, scaled, upper):
    def row_block(i, pos):
        bit = bit_of(pos, 0)
        return jnp.where(i < 2, 2 * (1 - bit), 2 * bit) + (i & 1)

    def body(blk_ref, pos_ref, x_ref, s_ref, u_ref, au, al, b0, b1, ks, kp, e_all):
        i = pl.program_id(0)
        rb = row_block(i, pos_ref)
        for b in range(4):
            e_all[b] = x_ref[0, :, b * 256 : (b + 1) * 256]
        subtract_product(
            blk_ref, pos_ref, 0, rb, lambda: s_ref[...], u_ref, e_all,
            lambda b, s: e_all[b].astype(F32),
        )
        nxt = col_pivot(blk_ref, pos_ref, 1)
        half = i & 1

        for n, b_ref in ((0, b0), (1, b1)):

            @pl.when(i == n)
            def _():
                al[n] = e_all[nxt]
                for d in range(3):
                    b_ref[d] = e_all[block_of(d, nxt)]

        @pl.when(i >= 2)
        def _():
            kp[half] = e_all[nxt]
            for d in range(3):
                ks[half, d] = e_all[block_of(d, nxt)]

        @pl.when(rb == row_pivot(blk_ref, pos_ref, 1))
        def _():
            for d in range(3):
                au[d] = e_all[block_of(d, nxt)]

    shapes = [
        (3, 256, 256), (2, 256, 256), (3, 256, 256), (3, 256, 256), (2, 3, 256, 256), (2, 256, 256),
    ]
    return call(
        body,
        (4,),
        [
            pl.BlockSpec((1, 256, 1024), lambda i, blk, pos: (0, row_block(i, pos), 0)),
            pl.BlockSpec(
                (256, 1024),
                lambda i, blk, pos: (slot_of(row_block(i, pos), row_pivot(blk, pos, 0)), 0),
            ),
            whole((3, 1024, 256)),
        ],
        [whole(x) for x in shapes],
        [out(x) for x in shapes],
        [pltpu.VMEM((4, 256, 256), BF)],
        flops=2 * 768 * 1024 * 768,
        size=8 * 2**20,
    )(blk, pos, tile, scaled, upper)


def update_second(blk, pos, ks, rb0, rb1, kp, ra, scaled, upper):
    def body(
        blk_ref, pos_ref, ks_ref, rb0_ref, rb1_ref, kp_ref, ra_ref, s_ref, u_ref,
        given, kept, al, bg, ks2, kp2, e_all,
    ):
        pivot = col_pivot(blk_ref, pos_ref, 1)
        nxt = col_pivot(blk_ref, pos_ref, 2)
        lead = bit_of(pos_ref, 0)
        for d in range(3):
            given[d] = jnp.zeros((128, 256), BF)
            kept[d] = jnp.zeros((128, 256), BF)
        for n, rb_ref in ((0, rb0_ref), (1, rb1_ref)):
            here = 2 * bit_of(pos_ref, 0) + n
            e_all[pivot] = (kp_ref[n].astype(F32) + ra_ref[n].astype(F32)).astype(BF)
            subtract_product(
                blk_ref, pos_ref, 1, here, lambda: s_ref[n * 256 : (n + 1) * 256], u_ref, e_all,
                lambda b, s: ks_ref[n, s].astype(F32) + rb_ref[s].astype(F32),
            )

            @pl.when(bit_of(pos_ref, 1) != n)
            def _():
                al[0] = e_all[nxt]
                for d in range(3):
                    bg[d] = e_all[block_of(d, nxt)]

            @pl.when(bit_of(pos_ref, 1) == n)
            def _():
                kp2[0] = e_all[nxt]
                for d in range(3):
                    ks2[d] = e_all[block_of(d, nxt)]

            @pl.when(here == row_pivot(blk_ref, pos_ref, 2))
            def _():
                for d in range(3):
                    given[d] = e_all[block_of(d, nxt), pl.ds((1 - lead) * 128, 128)]
                    kept[d] = e_all[block_of(d, nxt), pl.ds(lead * 128, 128)]

    shapes = [
        (3, 128, 256), (3, 128, 256), (1, 256, 256), (3, 256, 256), (3, 256, 256), (1, 256, 256),
    ]
    return call(
        body,
        (1,),
        [whole(x.shape) for x in (ks, rb0, rb1, kp, ra, scaled, upper)],
        [whole(x) for x in shapes],
        [out(x) for x in shapes],
        [pltpu.VMEM((4, 256, 256), BF)],
        flops=2 * 512 * 1024 * 768,
        size=7 * 2**20,
    )(blk, pos, ks, rb0, rb1, kp, ra, scaled, upper)


def update_third(blk, pos, ks, rb, kp, ra, scaled, upper):
    def body(
        blk_ref, pos_ref, ks_ref, rb_ref, kp_ref, ra_ref, s_ref, u_ref, give, keep, e_all
    ):
        here = 2 * bit_of(pos_ref, 0) + bit_of(pos_ref, 1)
        pivot = col_pivot(blk_ref, pos_ref, 2)
        e_all[pivot] = (kp_ref[0].astype(F32) + ra_ref[0].astype(F32)).astype(BF)
        subtract_product(
            blk_ref, pos_ref, 2, here, lambda: s_ref[...], u_ref, e_all,
            lambda b, s: ks_ref[s].astype(F32) + rb_ref[s].astype(F32),
        )
        bit = bit_of(pos_ref, 2)
        for b in range(4):
            give[:, b * 256 : (b + 1) * 256] = e_all[b, pl.ds((1 - bit) * 128, 128)]
            keep[:, b * 256 : (b + 1) * 256] = e_all[b, pl.ds(bit * 128, 128)]

    return call(
        body,
        (1,),
        [whole(x.shape) for x in (ks, rb, kp, ra, scaled, upper)],
        [whole((128, 1024)), whole((128, 1024))],
        [out((128, 1024)), out((128, 1024))],
        [pltpu.VMEM((4, 256, 256), BF)],
        flops=2 * 256 * 1024 * 768,
        size=4 * 2**20,
    )(blk, pos, ks, rb, kp, ra, scaled, upper)


def total(a, b):
    return (a.astype(F32) + b.astype(F32)).astype(BF)


def spread_rows(piece):
    near = row_swap(piece, True)
    far = row_swap(jnp.stack([piece, near]), False)
    return piece, near, far


def ring_rows(piece):
    rows = lax.axis_size("row")

    def step(n):
        route = lambda i: (i + n) % rows
        return move(piece, ("row",), route)

    return piece, step(2), step(1), step(3)


def gather_left(piece):
    both = jnp.stack([piece, far_half(piece)])
    return both, other_core(both)


def far_inverse(part):
    arrived = far_half(part)
    near = row_swap(arrived, True)
    two = jnp.stack([arrived, near])
    four = jnp.concatenate([two, row_swap(two, False)])
    return four, other_core(four)


def eliminate(schur, d_inv, blocks):
    row = lax.axis_index("row").astype(jnp.int32)
    blk = blocks[:, 0]
    pos = jnp.stack(
        [lax.axis_index("grid").astype(jnp.int32), row, lax.axis_index("col").astype(jnp.int32)]
    )
    inverse = d_inv.reshape(3, 4, 256, 256)
    left0, upper0, first, later = pack(blk, pos, schur, inverse)
    dz0, oz0 = far_inverse(first)
    d_other = other_core(inverse)
    upper0 = join_upper(blk, pos, spread_rows(upper0))
    lefts0 = gather_left(left0)
    dz12, oz12 = far_inverse(later)
    whole0 = join_inverse(blk, pos, (0, 1), inverse, dz0, d_other, oz0)
    whole12 = join_inverse(blk, pos, (1, 2), inverse, dz12, d_other, oz12)

    scaled0 = scale(blk, pos, 0, lefts0, whole0)
    au, al, b0, b1, ks, kp = update_first(blk, pos, schur, scaled0, upper0)
    ral = across(al, 1)
    upper1 = total(au, across(au, 1))
    rb0 = across(b0, 1)
    rb1 = across(b1, 1)
    upper1 = join_upper(blk, pos, spread_rows(upper1))
    lefts1 = gather_left(total(kp, ral))
    scaled1 = scale(blk, pos, 0, lefts1, whole12)
    given, kept, al, bg, ks, kp = update_second(
        blk, pos, ks, rb0, rb1, kp, ral, scaled1, upper1
    )

    ral = across(al, 2)
    rb = across(bg, 2)
    part = total(kept, across(given, 1))
    part = total(part, across(part, 2))
    upper2 = jnp.concatenate([part, across(part, 1)], axis=1)
    upper2 = join_upper(blk, pos, ring_rows(upper2), True)
    lefts2 = gather_left(total(kp, ral))
    scaled2 = scale(blk, pos, 1, lefts2, whole12)
    give, keep = update_third(blk, pos, ks, rb, kp, ral, scaled2, upper2)
    return total(keep, across(give, 4))[None]


def solution(mesh):
    return jax.shard_map(
        eliminate,
        mesh=mesh,
        in_specs=(P("grid", "row", "col"), P(None, "grid", None, "col"), P(None, "grid", None)),
        out_specs=P("grid", "row", "col"),
        check_vma=False,
    )
```

```python
import jax
import jax.numpy as jnp
from jax import lax
from jax.experimental import pallas as pl
from jax.experimental.pallas import tpu as pltpu
from jax.sharding import PartitionSpec as P


BF = jnp.bfloat16
F32 = jnp.float32


def move(block, axes, route):
    sizes = [lax.axis_size(a) for a in axes]
    count = 1
    for s in sizes:
        count *= s
    return lax.ppermute(block, axes, [(i, route(i)) for i in range(count)])


def across(block, apart):
    return move(block, ("grid",), lambda i: i ^ apart)


def far_half(block):
    return move(block, ("col",), lambda i: i ^ 2)


def other_core(block):
    return move(block, ("col",), lambda i: i ^ 1)


def row_swap(block, first):
    cols = lax.axis_size("col")

    def route(i):
        r, c = divmod(i, cols)
        mask = 1 if (c % 2 == 0) == first else 3
        return (r ^ mask) * cols + c

    return move(block, ("row", "col"), route)


def arrival(quarter, row, core):
    x = quarter ^ row
    near = jnp.where(core == 0, 3, 1)
    return jnp.where(x == 0, 0, jnp.where(x == 2, 3, jnp.where(x == near, 1, 2)))


def has(blk, level, wanted):
    found = blk[level, 0, 4] == wanted
    for n in range(5, 12):
        found = found | (blk[level, 0, n] == wanted)
    return found


def slot_of(b, pivot):
    return jnp.clip(b - jnp.where(b > pivot, 1, 0), 0, 2)


def block_of(slot, pivot):
    return slot + jnp.where(slot >= pivot, 1, 0)


def row_pivot(blk, pos, level):
    return blk[level, 0, pos[1]] - 4 * pos[1]


def col_pivot(blk, pos, level):
    return blk[level, 0, pos[2]] - 4 * pos[2]


def bit_of(pos, n):
    return (pos[0] >> n) & 1


def call(body, grid, in_specs, out_specs, out_shape, scratch, flops=0, size=0, limit=16):
    return pl.pallas_call(
        body,
        grid_spec=pltpu.PrefetchScalarGridSpec(
            num_scalar_prefetch=2,
            grid=grid,
            in_specs=in_specs,
            out_specs=out_specs,
            scratch_shapes=scratch,
        ),
        out_shape=out_shape,
        compiler_params=pltpu.CompilerParams(
            dimension_semantics=("arbitrary",) * len(grid), vmem_limit_bytes=int(limit * 2**20)
        ),
        cost_estimate=pl.CostEstimate(flops=flops, bytes_accessed=size, transcendentals=0),
    )


def whole(shape):
    return pl.BlockSpec(shape, lambda *_: (0,) * len(shape))


def out(shape):
    return jax.ShapeDtypeStruct(shape, BF)


def pack(blk, pos, tile, inverse):
    def body(blk_ref, pos_ref, x_ref, d_ref, left, upper, first, later, sems):
        row, col = row_pivot(blk_ref, pos_ref, 0), col_pivot(blk_ref, pos_ref, 0)

        def part(r, c):
            return x_ref.at[
                0, pl.ds(pl.multiple_of(r * 256, 256), 256), pl.ds(pl.multiple_of(c * 256, 256), 256)
            ]

        moves = [(d_ref.at[0, pos_ref[1]], first.at[0])]
        moves += [(part(block_of(i, row), col), left.at[i]) for i in range(3)]
        moves += [(part(row, block_of(i, col)), upper.at[i]) for i in range(3)]
        moves += [(d_ref.at[1 + i, pos_ref[1]], later.at[i]) for i in range(2)]
        copies = [
            pltpu.make_async_copy(src, dst, sems.at[n]) for n, (src, dst) in enumerate(moves)
        ]
        for copy in copies:
            copy.start()
        for copy in copies:
            copy.wait()

    shapes = [(3, 256, 256), (3, 256, 256), (1, 256, 256), (2, 256, 256)]
    return call(
        body,
        (1,),
        [pl.BlockSpec(memory_space=pltpu.HBM)] * 2,
        [whole(x) for x in shapes],
        [out(x) for x in shapes],
        [pltpu.SemaphoreType.DMA((9,))],
        size=2**21,
        limit=52,
    )(blk, pos, tile, inverse)


def join_inverse(blk, pos, levels, own, far, other, other_far):
    first, count = levels

    def body(blk_ref, pos_ref, dc, dz, oc, oz, d_ref):
        r, c = pos_ref[1], pos_ref[2]
        for k in range(4):
            rows = slice(k * 256, (k + 1) * 256)
            for flip, piece in (
                (0, dc[0, k]),
                (2, dz[arrival(k, r, c % 2), 0]),
                (1, oc[0, k]),
                (3, oz[arrival(k, r, (c % 2) ^ 1), 0]),
            ):
                d_ref[0, rows, pl.ds(pl.multiple_of((c ^ flip) * 256, 256), 256)] = piece

    near = pl.BlockSpec((1, 4, 256, 256), lambda n, blk, pos: (first + n, 0, 0, 0))
    swapped = pl.BlockSpec((4, 1, 256, 256), lambda n, blk, pos: (0, n, 0, 0))
    return call(
        body,
        (count,),
        [near, swapped, near, swapped],
        pl.BlockSpec((1, 1024, 1024), lambda n, blk, pos: (n, 0, 0)),
        out((count, 1024, 1024)),
        [],
        size=count * 2**22,
    )(blk, pos, own, far, other, other_far)


def join_upper(blk, pos, pieces, halved=False):
    def body(blk_ref, pos_ref, *refs):
        r, c = pos_ref[1], pos_ref[2]
        u_all = refs[-1]
        lead = bit_of(pos_ref, 0) * 128
        if len(refs) == 5:
            parts = tuple(((r + n) & 3, ref) for n, ref in zip((0, 2, 3, 1), refs))
        else:
            near_q = r ^ jnp.where(c % 2 == 0, 1, 3)
            far_q = r ^ jnp.where(c % 2 == 0, 3, 1)
            parts = (r, refs[0]), (near_q, refs[1]), (far_q, refs[2].at[0]), (r ^ 2, refs[2].at[1])
        for q, ref in parts:
            for s in range(3):
                if halved:
                    u_all[s, pl.ds(q * 256 + lead, 128)] = ref[s, :128]
                    u_all[s, pl.ds(q * 256 + 128 - lead, 128)] = ref[s, 128:]
                else:
                    u_all[s, pl.ds(q * 256, 256)] = ref[s]

    return call(
        body,
        (1,),
        [whole(x.shape) for x in pieces],
        whole((3, 1024, 256)),
        out((3, 1024, 256)),
        [],
        size=3 * 2**20,
    )(blk, pos, *pieces)


def scale(blk, pos, lane, lefts, inverse):
    rows = lefts[0].shape[1]

    def body(blk_ref, pos_ref, own, other, d_ref, s_ref, l_all):
        c = pos_ref[2]

        @pl.when(pl.program_id(0) == 0)
        def _():
            for flip, ref in zip((0, 2, 1, 3), (own.at[0], own.at[1], other.at[0], other.at[1])):
                for i in range(rows):
                    l_all[i * 256 : (i + 1) * 256, pl.ds(pl.multiple_of((c ^ flip) * 256, 256), 256)] = ref[i]

        s_ref[...] = jnp.dot(l_all[...], d_ref[0], preferred_element_type=F32).astype(BF)

    return call(
        body,
        (4,),
        [whole((2, rows, 256, 256))] * 2
        + [pl.BlockSpec((1, 1024, 256), lambda q, blk, pos: (lane, 0, q))],
        pl.BlockSpec((rows * 256, 256), lambda q, blk, pos: (0, q)),
        out((rows * 256, 1024)),
        [pltpu.VMEM((rows * 256, 1024), BF)],
        flops=2 * rows * 256 * 1024 * 1024,
        size=4 * 2**20,
    )(blk, pos, *lefts, inverse)


def subtract_product(blk_ref, pos_ref, level, row_block, scaled, u_ref, e_all, held):
    c = pos_ref[2]
    pivot = col_pivot(blk_ref, pos_ref, level)
    row_on = has(blk_ref, level, pos_ref[1] * 4 + row_block)
    for s in range(3):
        b = block_of(s, pivot)
        on = row_on & has(blk_ref, level, c * 4 + b)

        @pl.when(on)
        def _():
            change = jnp.dot(scaled(), u_ref[s], preferred_element_type=F32)
            e_all[b] = (held(b, s) - change).astype(BF)

        @pl.when(jnp.logical_not(on))
        def _():
            e_all[b] = held(b, s).astype(BF)


def scale_rows(pos_ref, lefts, d_ref, l_all, s_all):
    own, other = lefts
    c = pos_ref[2]
    for flip, ref in zip((0, 2, 1, 3), (own.at[0], own.at[1], other.at[0], other.at[1])):
        for i in range(ref.shape[0]):
            l_all[i * 256 : (i + 1) * 256, pl.ds(pl.multiple_of((c ^ flip) * 256, 256), 256)] = ref[i]
    for q in range(0, 1024, 256):
        s_all[:, q : q + 256] = jnp.dot(
            l_all[...], d_ref[0, :, q : q + 256], preferred_element_type=F32
        ).astype(BF)


def update_first(blk, pos, tile, lefts, inverse, upper):
    def row_block(i, pos):
        bit = bit_of(pos, 0)
        return jnp.where(i < 2, 2 * (1 - bit), 2 * bit) + (i & 1)

    def body(blk_ref, pos_ref, x_ref, own, other, d_ref, u_ref, au, al, b0, b1, ks, kp, e_all, l_all, s_all):
        i = pl.program_id(0)
        rb = row_block(i, pos_ref)
        for b in range(4):
            e_all[b] = x_ref[0, :, b * 256 : (b + 1) * 256]

        place = pl.multiple_of(slot_of(rb, row_pivot(blk_ref, pos_ref, 0)) * 256, 256)

        @pl.when(i == 0)
        def _():
            scale_rows(pos_ref, (own, other), d_ref, l_all, s_all)

        subtract_product(
            blk_ref, pos_ref, 0, rb, lambda: s_all[pl.ds(place, 256)], u_ref, e_all,
            lambda b, s: e_all[b].astype(F32),
        )
        nxt = col_pivot(blk_ref, pos_ref, 1)
        half = i & 1

        for n, b_ref in ((0, b0), (1, b1)):

            @pl.when(i == n)
            def _():
                al[n] = e_all[nxt]
                for d in range(3):
                    b_ref[d] = e_all[block_of(d, nxt)]

        @pl.when(i >= 2)
        def _():
            kp[half] = e_all[nxt]
            for d in range(3):
                ks[half, d] = e_all[block_of(d, nxt)]

        @pl.when(rb == row_pivot(blk_ref, pos_ref, 1))
        def _():
            for d in range(3):
                au[d] = e_all[block_of(d, nxt)]

    shapes = [
        (3, 256, 256), (2, 256, 256), (3, 256, 256), (3, 256, 256), (2, 3, 256, 256), (2, 256, 256),
    ]
    return call(
        body,
        (4,),
        [
            pl.BlockSpec((1, 256, 1024), lambda i, blk, pos: (0, row_block(i, pos), 0)),
            whole((2, 3, 256, 256)),
            whole((2, 3, 256, 256)),
            whole((1, 1024, 1024)),
            whole((3, 1024, 256)),
        ],
        [whole(x) for x in shapes],
        [out(x) for x in shapes],
        [pltpu.VMEM((4, 256, 256), BF), pltpu.VMEM((768, 1024), BF), pltpu.VMEM((768, 1024), BF)],
        flops=2 * 768 * 1024 * 1792,
        size=10 * 2**20,
        limit=24,
    )(blk, pos, tile, *lefts, inverse, upper)


def update_second(blk, pos, ks, rb0, rb1, kp, ra, lefts, inverse, upper):
    def body(
        blk_ref, pos_ref, ks_ref, rb0_ref, rb1_ref, kp_ref, ra_ref, own, other, d_ref, u_ref,
        given, kept, al, bg, ks2, kp2, e_all, l_all, s_all,
    ):
        pivot = col_pivot(blk_ref, pos_ref, 1)
        nxt = col_pivot(blk_ref, pos_ref, 2)
        lead = bit_of(pos_ref, 0)
        for d in range(3):
            given[d] = jnp.zeros((128, 256), BF)
            kept[d] = jnp.zeros((128, 256), BF)
        scale_rows(pos_ref, (own, other), d_ref, l_all, s_all)
        for n, rb_ref in ((0, rb0_ref), (1, rb1_ref)):
            here = 2 * bit_of(pos_ref, 0) + n
            e_all[pivot] = (kp_ref[n].astype(F32) + ra_ref[n].astype(F32)).astype(BF)

            subtract_product(
                blk_ref, pos_ref, 1, here, lambda: s_all[n * 256 : (n + 1) * 256], u_ref, e_all,
                lambda b, s: ks_ref[n, s].astype(F32) + rb_ref[s].astype(F32),
            )

            @pl.when(bit_of(pos_ref, 1) != n)
            def _():
                al[0] = e_all[nxt]
                for d in range(3):
                    bg[d] = e_all[block_of(d, nxt)]

            @pl.when(bit_of(pos_ref, 1) == n)
            def _():
                kp2[0] = e_all[nxt]
                for d in range(3):
                    ks2[d] = e_all[block_of(d, nxt)]

            @pl.when(here == row_pivot(blk_ref, pos_ref, 2))
            def _():
                for d in range(3):
                    given[d] = e_all[block_of(d, nxt), pl.ds((1 - lead) * 128, 128)]
                    kept[d] = e_all[block_of(d, nxt), pl.ds(lead * 128, 128)]

    shapes = [
        (3, 128, 256), (3, 128, 256), (1, 256, 256), (3, 256, 256), (3, 256, 256), (1, 256, 256),
    ]
    return call(
        body,
        (1,),
        [whole(x.shape) for x in (ks, rb0, rb1, kp, ra, *lefts)]
        + [pl.BlockSpec((1, 1024, 1024), lambda i, blk, pos: (0, 0, 0)), whole(upper.shape)],
        [whole(x) for x in shapes],
        [out(x) for x in shapes],
        [pltpu.VMEM((4, 256, 256), BF), pltpu.VMEM((512, 1024), BF), pltpu.VMEM((512, 1024), BF)],
        flops=2 * 512 * 1024 * 1792,
        size=9 * 2**20,
        limit=24,
    )(blk, pos, ks, rb0, rb1, kp, ra, *lefts, inverse, upper)


def update_third(blk, pos, ks, rb, kp, ra, scaled, upper):
    def body(
        blk_ref, pos_ref, ks_ref, rb_ref, kp_ref, ra_ref, s_ref, u_ref, give, keep, e_all
    ):
        here = 2 * bit_of(pos_ref, 0) + bit_of(pos_ref, 1)
        pivot = col_pivot(blk_ref, pos_ref, 2)
        e_all[pivot] = (kp_ref[0].astype(F32) + ra_ref[0].astype(F32)).astype(BF)
        subtract_product(
            blk_ref, pos_ref, 2, here, lambda: s_ref[...], u_ref, e_all,
            lambda b, s: ks_ref[s].astype(F32) + rb_ref[s].astype(F32),
        )
        bit = bit_of(pos_ref, 2)
        for b in range(4):
            give[:, b * 256 : (b + 1) * 256] = e_all[b, pl.ds((1 - bit) * 128, 128)]
            keep[:, b * 256 : (b + 1) * 256] = e_all[b, pl.ds(bit * 128, 128)]

    return call(
        body,
        (1,),
        [whole(x.shape) for x in (ks, rb, kp, ra, scaled, upper)],
        [whole((128, 1024)), whole((128, 1024))],
        [out((128, 1024)), out((128, 1024))],
        [pltpu.VMEM((4, 256, 256), BF)],
        flops=2 * 256 * 1024 * 768,
        size=4 * 2**20,
    )(blk, pos, ks, rb, kp, ra, scaled, upper)


def total(a, b):
    return (a.astype(F32) + b.astype(F32)).astype(BF)


def spread_rows(piece):
    near = row_swap(piece, True)
    far = row_swap(jnp.stack([piece, near]), False)
    return piece, near, far


def ring_rows(piece):
    rows = lax.axis_size("row")

    def step(n):
        route = lambda i: (i + n) % rows
        return move(piece, ("row",), route)

    return piece, step(2), step(1), step(3)


def gather_left(piece):
    both = jnp.stack([piece, far_half(piece)])
    return both, other_core(both)


def far_inverse(part):
    arrived = far_half(part)
    near = row_swap(arrived, False)
    two = jnp.stack([arrived, near])
    four = jnp.concatenate([two, row_swap(two, True)])
    return four, other_core(four)


def eliminate(schur, d_inv, blocks):
    row = lax.axis_index("row").astype(jnp.int32)
    blk = blocks
    pos = jnp.stack(
        [lax.axis_index("grid").astype(jnp.int32), row, lax.axis_index("col").astype(jnp.int32)]
    )
    inverse = d_inv.reshape(3, 4, 256, 256)
    left0, upper0, first, later = pack(blk, pos, schur, inverse)
    dz0, oz0 = far_inverse(first)
    d_other = other_core(inverse)
    upper0 = join_upper(blk, pos, spread_rows(upper0))
    lefts0 = gather_left(left0)
    dz12, oz12 = far_inverse(later)
    whole0 = join_inverse(blk, pos, (0, 1), inverse, dz0, d_other, oz0)
    whole12 = join_inverse(blk, pos, (1, 2), inverse, dz12, d_other, oz12)

    au, al, b0, b1, ks, kp = update_first(blk, pos, schur, lefts0, whole0, upper0)
    ral = across(al, 1)
    upper1 = total(au, across(au, 1))
    rb0 = across(b0, 1)
    rb1 = across(b1, 1)
    upper1 = join_upper(blk, pos, spread_rows(upper1))
    lefts1 = gather_left(total(kp, ral))
    given, kept, al, bg, ks, kp = update_second(
        blk, pos, ks, rb0, rb1, kp, ral, lefts1, whole12, upper1
    )

    ral = across(al, 2)
    rb = across(bg, 2)
    part = total(kept, across(given, 1))
    part = total(part, across(part, 2))
    upper2 = jnp.concatenate([part, across(part, 1)], axis=1)
    upper2 = join_upper(blk, pos, ring_rows(upper2), True)
    lefts2 = gather_left(total(kp, ral))
    scaled2 = scale(blk, pos, 1, lefts2, whole12)
    give, keep = update_third(blk, pos, ks, rb, kp, ral, scaled2, upper2)
    return total(keep, across(give, 4))[None]


def solution(mesh):
    return jax.shard_map(
        eliminate,
        mesh=mesh,
        in_specs=(P("grid", "row", "col"), P(None, "grid", None, "col"), P(None, "grid", None)),
        out_specs=P("grid", "row", "col"),
        check_vma=False,
    )
```
